32 devices in a mesh: grp: 4 (over x, core), inf: 8 (over z, y).
Axes of the slice: x: 2, y: 2, z: 4, core: 2. Of those that a mesh axis runs over, the one named last changes fastest.
Arguments:
- range_one: float32 [1408], replicated, may hold values from 0.05 to 1
- range_two: float32 [1408], replicated, may hold values from 0.05 to 1
- flop_weight: int32 [1024], P('grp'), may hold values from 0 to 24, as said below
- board_mask: int32 [1024, 1408], P('grp', 'inf'), may hold values 0 or 1
- runout: int32 [1024, 4, 2], P('grp'), may hold values from 0 to 51
- strength: int32 [1024, 4, 1408], P('grp', None, 'inf'), may hold values from 0 to 1073741823
Outputs:
- turn_reach: float32 [512, 6, 1408], P(('grp', 'inf'))
- preflop_reach: float32 [1408], P('inf')
The draws below stay inside these ranges and needn't reach their ends.
Inputs may be any that keep to these rules, and one draw needn't show every extreme that they name: `flop_weight`: slots 256 g to 256 g + 255 belong to group g; in each group the slots with nonzero weight come first; nonzero weights are 4, 12 or 24; exactly 512 slots in all have nonzero weight, every group has at least half of 128 of them, and the busiest group has exactly 256.
All inputs are finite; a program needn't handle non-finite values. No bound on the sum of `board_mask` on one device may be relied on, other than what follows from the above.
Results may differ from the reference program's by a relative error of at most 0.0003.
Values may be sent and summed in bfloat16 or wider, within the bound.
A program may use at most 64 MiB of HBM per device.

```python
from functools import partial
import jax
import jax.numpy as jnp
import numpy as np
from jax import lax

HANDS = 1326
H = 1408
ITERS = 4
FLOP_GRP = 128
CAP = 256
FLOPS = 512
SLOTS = 1024
N_GRP = 4


def draw_flop_weight(key, part):
    shift_key = jax.random.fold_in(key, 11)
    first_key = jax.random.fold_in(key, 12)
    second_key = jax.random.fold_in(key, 14)
    kind_key = jax.random.fold_in(key, 13)
    shift = jax.random.randint(shift_key, (), 0, 4)
    first_extra = jax.random.randint(first_key, (), 0, FLOP_GRP // 4 + 1)
    second_extra = jax.random.randint(second_key, (), 0, FLOP_GRP // 4 + 1)
    base_counts = jnp.stack([jnp.asarray(CAP, jnp.int32), FLOP_GRP // 2 + first_extra, FLOP_GRP // 2 + second_extra, FLOP_GRP - first_extra - second_extra]).astype(jnp.int32)
    group_ids = jnp.arange(4)
    counts = base_counts[(group_ids - shift) % 4]
    slot_ids = jnp.arange(SLOTS)
    slot_group = slot_ids // CAP
    slot_place = slot_ids % CAP
    is_live = slot_place < counts[slot_group]
    kind_ids = jax.random.randint(kind_key, (SLOTS,), 0, 3)
    multiplicity = jnp.where(kind_ids == 0, 4, jnp.where(kind_ids == 1, 12, 24))
    return jnp.where(is_live, multiplicity, 0).astype(jnp.int32)


def set_ends(entries, rng, smallest, largest):
    spot = [jax.random.randint(jax.random.fold_in(rng, axis), (), 0, length) for axis, length in enumerate(entries.shape)]
    widest = entries.shape.index(max(entries.shape))
    next_to = spot[:widest] + [(spot[widest] + 1) % entries.shape[widest]] + spot[widest + 1:]
    return entries.at[tuple(spot)].set(smallest).at[tuple(next_to)].set(largest)


def setup_inputs(seed: int = 0) -> dict:
    splits = jax.random.split(jax.random.key(seed), 7)
    range_one = jnp.clip(jax.random.uniform(splits[0], (H,), jnp.float32, 0.05, 1.0), 0.05, 1.0)
    range_two = jnp.clip(jax.random.uniform(splits[1], (H,), jnp.float32, 0.05, 1.0), 0.05, 1.0)
    flop_weight = draw_flop_weight(jax.random.fold_in(splits[6], 71), 0)
    board_mask = set_ends((jax.random.randint(splits[3], (SLOTS, H), 0, 9) < 8).astype(jnp.int32), jax.random.fold_in(splits[3], 1), 0, 1)
    runout = set_ends(jax.random.randint(splits[4], (SLOTS, ITERS, 2), 0, 52), jax.random.fold_in(splits[4], 1), 0, 51).astype(jnp.int32)
    strength = set_ends(jax.random.randint(splits[5], (SLOTS, ITERS, H), 0, 1073741824), jax.random.fold_in(splits[5], 1), 0, 1073741823).astype(jnp.int32)
    return {"range_one": range_one, "range_two": range_two, "flop_weight": flop_weight, "board_mask": board_mask, "runout": runout, "strength": strength}


EPSILON = 0.01
FOLD_VALUE = -0.1


def hand_cards(slot_total, real_total):
    low_list = []
    high_list = []
    for first_card in range(52):
        for second_card in range(first_card + 1, 52):
            low_list.append(first_card)
            high_list.append(second_card)
    low_table = np.full(slot_total, 52, np.int32)
    high_table = np.full(slot_total, 53, np.int32)
    used_count = min(slot_total, real_total)
    low_table[:used_count] = np.array(low_list[:used_count], np.int32)
    high_table[:used_count] = np.array(high_list[:used_count], np.int32)
    return low_table, high_table


def action_share(first_regret, second_regret):
    return (first_regret + EPSILON) / (first_regret + second_regret + 2.0 * EPSILON)


def slot_values(low_card, high_card, member):
    key_row, reach_columns = member
    compat = (low_card[:, None] != low_card[None, :]) & (low_card[:, None] != high_card[None, :])
    compat = compat & (high_card[:, None] != low_card[None, :]) & (high_card[:, None] != high_card[None, :])
    both_live = compat & (key_row[:, None] >= 0) & (key_row[None, :] >= 0)
    weight_mat = both_live.astype(jnp.bfloat16)
    sign_mat = jnp.sign(key_row[:, None] - key_row[None, :]).astype(jnp.bfloat16) * weight_mat
    sign_sum = jnp.dot(reach_columns, sign_mat.T, preferred_element_type=jnp.float32)
    summed_weight_total = jnp.dot(reach_columns, weight_mat.T, preferred_element_type=jnp.float32)
    return sign_sum, summed_weight_total


def reference(range_one, range_two, flop_weight, board_mask, runout, strength):
    low_table, high_table = hand_cards(H, HANDS)
    low_card = jnp.asarray(low_table)
    high_card = jnp.asarray(high_table)
    slot_all = jnp.arange(SLOTS).astype(jnp.int32)
    slot_group = slot_all // CAP
    slot_place = slot_all % CAP
    order_key = jnp.where(flop_weight > 0, slot_place * N_GRP + slot_group, CAP * N_GRP + slot_all).astype(jnp.int32)
    live_slots = jnp.argsort(order_key)[:FLOPS].astype(jnp.int32)
    flop_share = flop_weight[live_slots].astype(jnp.float32) / (12.0 * FLOPS)
    board_rows = board_mask[live_slots]
    run_cards = runout[live_slots]
    key_rows = strength[live_slots]
    slot_ids = jnp.arange(H)
    flop_live = ((board_rows == 1) & (slot_ids < HANDS)[None, :]).astype(jnp.float32)
    payoff_value_scale = 1.0 / HANDS
    player_two_total = range_two[None, :] * flop_live
    zero_flop = jnp.zeros((FLOPS, H), jnp.float32)
    root_check = root_bet = facing_call_fold = fc_call = zero_flop
    ac_check = ac_bet = fb_fold = fb_call = zero_flop
    pre_fold = jnp.zeros((H,), jnp.float32)
    pre_cont = jnp.zeros((H,), jnp.float32)
    turn_sum = jnp.zeros((FLOPS, 6, H), jnp.float32)
    pre_sum = jnp.zeros((H,), jnp.float32)
    for counter in range(ITERS):
        share_pre = action_share(pre_cont, pre_fold)
        one_range = range_one * share_pre
        player_one_total = one_range[None, :] * flop_live
        share_root = action_share(root_check, root_bet)
        facing_call_share = action_share(facing_call_fold, fc_call)
        share_ac = action_share(ac_check, ac_bet)
        share_fb = action_share(fb_fold, fb_call)
        player_one_check_share = player_one_total * share_root
        player_one_check_bet_fold = player_one_check_share * facing_call_share
        player_two_check_check = player_two_total * share_ac
        player_two_bet_fold = player_two_total * share_fb
        reach_columns = jnp.stack([player_two_total, player_two_check_check, player_two_bet_fold, player_one_total, player_one_check_share, player_one_check_bet_fold], axis=1).astype(jnp.bfloat16)
        turn_card = run_cards[:, counter, 0:1]
        river_card = run_cards[:, counter, 1:2]
        blocked = (low_card[None, :] == turn_card) | (low_card[None, :] == river_card)
        blocked = blocked | (high_card[None, :] == turn_card) | (high_card[None, :] == river_card)
        is_alive = (flop_live > 0) & jnp.logical_not(blocked)
        key_now = jnp.where(is_alive, key_rows[:, counter, :], -1).astype(jnp.int32)
        sign_sum, summed_weight_total = lax.map(partial(slot_values, low_card, high_card), (key_now, reach_columns))
        v_cc = 0.5 * payoff_value_scale * sign_sum[:, 1, :]
        check_bet_fold_value = -0.5 * payoff_value_scale * (summed_weight_total[:, 0, :] - summed_weight_total[:, 1, :])
        check_bet_call_value = 1.5 * payoff_value_scale * (sign_sum[:, 0, :] - sign_sum[:, 1, :])
        v_bf = 0.5 * payoff_value_scale * summed_weight_total[:, 2, :]
        v_bc = 1.5 * payoff_value_scale * (sign_sum[:, 0, :] - sign_sum[:, 2, :])
        w_cc = 0.5 * payoff_value_scale * sign_sum[:, 4, :]
        check_bet_fold_weight = 0.5 * payoff_value_scale * summed_weight_total[:, 5, :]
        check_bet_call_weight = 1.5 * payoff_value_scale * (sign_sum[:, 4, :] - sign_sum[:, 5, :])
        w_bf = -0.5 * payoff_value_scale * (summed_weight_total[:, 3, :] - summed_weight_total[:, 4, :])
        w_bc = 1.5 * payoff_value_scale * (sign_sum[:, 3, :] - sign_sum[:, 4, :])
        facing_call_utility = facing_call_share * check_bet_fold_value + (1.0 - facing_call_share) * check_bet_call_value
        v_check = v_cc + facing_call_utility
        v_bet = v_bf + v_bc
        u_root = share_root * v_check + (1.0 - share_root) * v_bet
        strategy_bet_share = check_bet_fold_weight + check_bet_call_weight
        u_ac = share_ac * w_cc + (1.0 - share_ac) * strategy_bet_share
        u_fb = share_fb * w_bf + (1.0 - share_fb) * w_bc
        facing_call_fold = jnp.maximum(facing_call_fold + check_bet_fold_value - facing_call_utility, 0.0)
        fc_call = jnp.maximum(fc_call + check_bet_call_value - facing_call_utility, 0.0)
        root_check = jnp.maximum(root_check + v_check - u_root, 0.0)
        root_bet = jnp.maximum(root_bet + v_bet - u_root, 0.0)
        ac_check = jnp.maximum(ac_check + w_cc - u_ac, 0.0)
        ac_bet = jnp.maximum(ac_bet + strategy_bet_share - u_ac, 0.0)
        fb_fold = jnp.maximum(fb_fold + w_bf - u_fb, 0.0)
        fb_call = jnp.maximum(fb_call + w_bc - u_fb, 0.0)
        cont_value = jnp.sum(flop_share[:, None] * u_root, axis=0)
        u_pre = share_pre * cont_value + (1.0 - share_pre) * FOLD_VALUE
        pre_cont = jnp.maximum(pre_cont + cont_value - u_pre, 0.0)
        pre_fold = jnp.maximum(pre_fold + FOLD_VALUE - u_pre, 0.0)
        iter_weight = float(counter + 1)
        turn_row_block = jnp.stack([player_one_check_share, player_one_total - player_one_check_share, player_one_check_share - player_one_check_bet_fold, player_two_check_check, player_two_total - player_two_bet_fold, player_two_total - player_two_check_check], axis=1)
        turn_sum = turn_sum + iter_weight * turn_row_block
        pre_sum = pre_sum + iter_weight * one_range
    total_weight = ITERS * (ITERS + 1) / 2.0
    return turn_sum / total_weight, pre_sum / total_weight
```

```python
import functools

import jax
import jax.numpy as jnp
import numpy as np
from jax import lax
from jax.experimental import pallas as pl
from jax.experimental.pallas import tpu as pltpu
from jax.sharding import PartitionSpec as P

HANDS = 1326
H = 1408
ITERS = 4
FLOP_GRP = 128


EPSILON = 0.01
FOLD_VALUE = -0.1
BLOCK = 256


def hand_cards(slot_total, real_total):
    low_list = []
    high_list = []
    for first_card in range(52):
        for second_card in range(first_card + 1, 52):
            low_list.append(first_card)
            high_list.append(second_card)
    low_table = np.full(slot_total, 52, np.int32)
    high_table = np.full(slot_total, 53, np.int32)
    used_count = min(slot_total, real_total)
    low_table[:used_count] = np.array(low_list[:used_count], np.int32)
    high_table[:used_count] = np.array(high_list[:used_count], np.int32)
    return (low_table, high_table)


def action_share(first_regret, second_regret):
    return (first_regret + EPSILON) / (first_regret + second_regret + 2.0 * EPSILON)


def order_floats(key):
    centred = key - (1 << 29)
    size = jnp.where(centred >= 0, centred, -1 - centred)
    power = size >> 23
    value = ((size & ((1 << 23) - 1)) + (1 << 23)).astype(jnp.float32)
    for bit in range(6):
        value = value * jnp.where((power >> bit) & 1 == 1, float(2 ** (2**bit)), 1.0)
    return jnp.where(centred >= 0, value, -value)


ROOT_CHECK, ROOT_BET, FC_FOLD, FC_CALL, AC_CHECK, AC_BET, FB_FOLD, FB_CALL = range(8)


def reaches(regrets, one_range, range_two, live):
    share_root = action_share(regrets[ROOT_CHECK], regrets[ROOT_BET])
    share_fc = action_share(regrets[FC_FOLD], regrets[FC_CALL])
    share_ac = action_share(regrets[AC_CHECK], regrets[AC_BET])
    share_fb = action_share(regrets[FB_FOLD], regrets[FB_CALL])
    one_all = one_range * live
    one_check = one_all * share_root
    one_cbf = one_check * share_fc
    two_all = range_two * live
    two_cc = two_all * share_ac
    two_bf = two_all * share_fb
    shares = (share_root, share_fc, share_ac, share_fb)
    return shares, (two_all, two_cc, two_bf, one_all, one_check, one_cbf)


def turn_rows(cols):
    two_all, two_cc, two_bf, one_all, one_check, one_cbf = cols
    return (
        one_check,
        one_all - one_check,
        one_check - one_cbf,
        two_cc,
        two_all - two_bf,
        two_all - two_cc,
    )


def step_kernel(
    step,
    compat_ref,
    order_ref,
    live_ref,
    alive_ref,
    share_ref,
    one_ref,
    two_ref,
    *rest,
):
    if step == 0:
        regret_out, turn_out, cont_ref, minus_ref, cols_ref, sign_ref, weight_ref = rest
        regrets = [jnp.zeros(live_ref.shape, jnp.float32)] * 8
    else:
        (
            regret_in,
            turn_in,
            regret_out,
            turn_out,
            cont_ref,
            minus_ref,
            cols_ref,
            sign_ref,
            weight_ref,
        ) = rest
        regrets = [regret_in[row] for row in range(8)]
    slots, width = live_ref.shape
    live = live_ref[...]
    alive = alive_ref[...]
    shares, cols = reaches(regrets, one_ref[...], two_ref[...], live)
    iter_weight = float(step + 1)
    for row, term in enumerate(turn_rows(cols)):
        if step == 0:
            turn_out[row] = iter_weight * term
        else:
            turn_out[row] = turn_in[row] + iter_weight * term
    for row in range(6):
        cols_ref[:, row, :] = cols[row].astype(jnp.bfloat16).astype(jnp.float32) * alive
    for row in range(6, 8):
        cols_ref[:, row, :] = jnp.zeros_like(alive)
    minus_ref[...] = -compat_ref[...]

    def one_flop(slot, carry):
        mine = order_ref[pl.ds(slot, 1), :]
        cols_now = cols_ref[slot].astype(jnp.bfloat16)
        total = jnp.zeros((8, width), jnp.float32)
        for first in range(0, width, BLOCK):
            last = min(first + BLOCK, width)
            theirs = jnp.concatenate(
                [
                    jnp.transpose(jnp.broadcast_to(mine[:, spot : spot + 128], (128, 128)))
                    for spot in range(first, last, 128)
                ],
                axis=0,
            )
            blocks = []
            for spot in range(0, width, 128):
                gap = (mine[:, spot : spot + 128] - theirs).astype(jnp.bfloat16)
                limit = compat_ref[first:last, spot : spot + 128]
                blocks.append(
                    jnp.minimum(
                        jnp.maximum(gap, minus_ref[first:last, spot : spot + 128]), limit
                    )
                )
            sign_block = jnp.concatenate(blocks, axis=1)
            total = total + jnp.dot(
                cols_now[:, first:last], sign_block, preferred_element_type=jnp.float32
            )
        sign_ref[slot] = total
        return carry

    lax.fori_loop(0, slots, one_flop, 0)
    all_cols = cols_ref[...].reshape(slots * 8, width).astype(jnp.bfloat16)
    weight_ref[...] = jnp.dot(
        all_cols, compat_ref[...], preferred_element_type=jnp.float32
    ).reshape(slots, 8, width)

    share_root, share_fc, share_ac, share_fb = shares
    scale = 1.0 / HANDS
    sv = [sign_ref[:, row, :] * alive for row in range(6)]
    wv = [weight_ref[:, row, :] * alive for row in range(6)]
    v_cc = 0.5 * scale * sv[1]
    v_cbf = -0.5 * scale * (wv[0] - wv[1])
    v_cbc = 1.5 * scale * (sv[0] - sv[1])
    v_bf = 0.5 * scale * wv[2]
    v_bc = 1.5 * scale * (sv[0] - sv[2])
    w_cc = 0.5 * scale * sv[4]
    w_cbf = 0.5 * scale * wv[5]
    w_cbc = 1.5 * scale * (sv[4] - sv[5])
    w_bf = -0.5 * scale * (wv[3] - wv[4])
    w_bc = 1.5 * scale * (sv[3] - sv[4])
    u_fc = share_fc * v_cbf + (1.0 - share_fc) * v_cbc
    v_check = v_cc + u_fc
    v_bet = v_bf + v_bc
    u_root = share_root * v_check + (1.0 - share_root) * v_bet
    x_bet = w_cbf + w_cbc
    u_ac = share_ac * w_cc + (1.0 - share_ac) * x_bet
    u_fb = share_fb * w_bf + (1.0 - share_fb) * w_bc
    updates = (
        (ROOT_CHECK, v_check, u_root),
        (ROOT_BET, v_bet, u_root),
        (FC_FOLD, v_cbf, u_fc),
        (FC_CALL, v_cbc, u_fc),
        (AC_CHECK, w_cc, u_ac),
        (AC_BET, x_bet, u_ac),
        (FB_FOLD, w_bf, u_fb),
        (FB_CALL, w_bc, u_fb),
    )
    for row, value, node in updates:
        regret_out[row] = jnp.maximum(regrets[row] + value - node, 0.0)
    cont_ref[...] = jnp.sum(share_ref[...] * u_root, axis=0, keepdims=True)


def run_step(step, *operands):
    slots, width = operands[1].shape
    vmem = pl.BlockSpec(memory_space=pltpu.VMEM)
    return pl.pallas_call(
        functools.partial(step_kernel, step),
        out_shape=(
            jax.ShapeDtypeStruct((8, slots, width), jnp.float32),
            jax.ShapeDtypeStruct((6, slots, width), jnp.float32),
            jax.ShapeDtypeStruct((1, width), jnp.float32),
        ),
        in_specs=[vmem] * len(operands),
        out_specs=(vmem,) * 3,
        scratch_shapes=[
            pltpu.VMEM((width, width), jnp.bfloat16),
            pltpu.VMEM((slots, 8, width), jnp.float32),
            pltpu.VMEM((slots, 8, width), jnp.float32),
            pltpu.VMEM((slots, 8, width), jnp.float32),
        ],
        compiler_params=pltpu.CompilerParams(vmem_limit_bytes=56 * 1024 * 1024),
    )(*operands)


def on_device(range_one, range_two, flop_weight, board_mask, runout, strength):
    groups = lax.axis_size("grp")
    shards = lax.axis_size("inf")
    shard_id = lax.axis_index("inf")
    group_id = lax.axis_index("grp")
    low_table, high_table = hand_cards(H, HANDS)
    low_all = jnp.asarray(low_table)
    high_all = jnp.asarray(high_table)
    capacity = strength.shape[0]
    hand_block = strength.shape[2]
    flop_total = 12.0 * FLOP_GRP * groups
    rounds = ITERS - 1
    local_count = FLOP_GRP // shards

    small = jnp.concatenate(
        [flop_weight[:, None], runout[:, :rounds].reshape(capacity, 2 * rounds)], axis=1
    )
    small_all = lax.all_gather(small, "grp", axis=0, tiled=False)
    counts = jnp.sum((small_all[:, :, 0] > 0).astype(jnp.int32), axis=1, dtype=jnp.int32)
    rows = jnp.arange(capacity)
    group_ids = jnp.arange(groups)
    earlier = (group_ids[None, :] < group_ids[:, None]).astype(jnp.int32)
    place = jnp.sum(
        jnp.minimum(counts[None, None, :], rows[None, :, None] + earlier[:, None, :]),
        axis=2,
        dtype=jnp.int32,
    )
    place = jnp.where(rows[None, :] < counts[:, None], place, -1)

    masked = jnp.where(board_mask[:, None, :] == 1, strength[:, :rounds], -1)
    masked = masked.reshape(capacity, rounds * hand_block)
    own_place = jnp.sum(
        jnp.where(group_ids[:, None] == group_id, place, 0), axis=0, dtype=jnp.int32
    )
    target = jnp.arange(groups * FLOP_GRP)
    match = own_place[None, :] == target[:, None]
    is_valid = jnp.any(match, axis=1)
    source = jnp.sum(jnp.where(match, rows[None, :], 0), axis=1, dtype=jnp.int32)
    taken = jnp.where(is_valid[:, None], jnp.take(masked, source, axis=0), 0)
    arrived = lax.all_to_all(
        taken.reshape(groups, FLOP_GRP, rounds * hand_block),
        "grp",
        split_axis=0,
        concat_axis=0,
        tiled=True,
    )
    key_rows = jnp.sum(arrived, axis=0, dtype=jnp.int32).reshape(FLOP_GRP, rounds, hand_block)
    flop_keys = lax.all_to_all(key_rows, "inf", split_axis=0, concat_axis=2, tiled=True)

    here = group_id * FLOP_GRP + shard_id * local_count + jnp.arange(local_count)
    mine = place.reshape(1, -1) == here[:, None]
    small_here = jnp.sum(
        jnp.where(mine[:, :, None], small_all.reshape(1, groups * capacity, -1), 0),
        axis=1,
        dtype=jnp.int32,
    )
    flop_share = small_here[:, 0:1].astype(jnp.float32) / flop_total

    is_hand = (jnp.arange(H) < HANDS)[None, :]
    is_live = (flop_keys[:, 0, :] >= 0) & is_hand
    live = is_live.astype(jnp.float32)
    compat = (low_all[:, None] != low_all[None, :]) & (low_all[:, None] != high_all[None, :])
    compat = compat & (high_all[:, None] != low_all[None, :])
    compat = compat & (high_all[:, None] != high_all[None, :])
    compat = compat.astype(jnp.bfloat16)

    two_row = range_two[None, :]
    pre_fold = jnp.zeros((1, H), jnp.float32)
    pre_cont = jnp.zeros((1, H), jnp.float32)
    pre_sum = jnp.zeros((1, H), jnp.float32)
    state = ()
    for step in range(rounds):
        share_pre = action_share(pre_cont, pre_fold)
        one_range = range_one[None, :] * share_pre
        turn_card = small_here[:, 1 + 2 * step : 2 + 2 * step]
        river_card = small_here[:, 2 + 2 * step : 3 + 2 * step]
        blocked = (low_all[None, :] == turn_card) | (low_all[None, :] == river_card)
        blocked = blocked | (high_all[None, :] == turn_card) | (high_all[None, :] == river_card)
        alive = (is_live & jnp.logical_not(blocked)).astype(jnp.float32)
        regrets, turn_sum, cont_part = run_step(
            step,
            compat,
            order_floats(jnp.maximum(flop_keys[:, step, :], 0)),
            live,
            alive,
            flop_share,
            one_range,
            two_row,
            *state,
        )
        state = (regrets, turn_sum)
        cont_value = lax.psum(cont_part, ("grp", "inf"))
        u_pre = share_pre * cont_value + (1.0 - share_pre) * FOLD_VALUE
        pre_cont = jnp.maximum(pre_cont + cont_value - u_pre, 0.0)
        pre_fold = jnp.maximum(pre_fold + FOLD_VALUE - u_pre, 0.0)
        pre_sum = pre_sum + float(step + 1) * one_range
    total_weight = ITERS * (ITERS + 1) / 2.0
    one_range = range_one[None, :] * action_share(pre_cont, pre_fold)
    unused, cols = reaches([state[0][row] for row in range(8)], one_range, two_row, live)
    turn_final = jnp.stack(
        [
            (state[1][row] + float(ITERS) * term) / total_weight
            for row, term in enumerate(turn_rows(cols))
        ],
        axis=1,
    )
    pre_sum = (pre_sum + float(ITERS) * one_range) / total_weight
    pre_block = lax.dynamic_slice_in_dim(pre_sum[0], shard_id * hand_block, hand_block)
    return (turn_final, pre_block)


def solution(mesh):
    in_specs = (P(), P(), P("grp"), P("grp", "inf"), P("grp", None, None), P("grp", None, "inf"))
    out_specs = (P(("grp", "inf"), None, None), P("inf"))
    return jax.shard_map(
        on_device, mesh=mesh, in_specs=in_specs, out_specs=out_specs, check_vma=False
    )
```

```python
import functools

import jax
import jax.numpy as jnp
import numpy as np
from jax import lax
from jax.experimental import pallas as pl
from jax.experimental.pallas import tpu as pltpu
from jax.sharding import PartitionSpec as P

HANDS = 1326
H = 1408
ITERS = 4
FLOP_GRP = 128


EPSILON = 0.01
FOLD_VALUE = -0.1
BLOCK = 256


def hand_cards(slot_total, real_total):
    low_list = []
    high_list = []
    for first_card in range(52):
        for second_card in range(first_card + 1, 52):
            low_list.append(first_card)
            high_list.append(second_card)
    low_table = np.full(slot_total, 52, np.int32)
    high_table = np.full(slot_total, 53, np.int32)
    used_count = min(slot_total, real_total)
    low_table[:used_count] = np.array(low_list[:used_count], np.int32)
    high_table[:used_count] = np.array(high_list[:used_count], np.int32)
    return (low_table, high_table)


def action_share(first_regret, second_regret):
    return (first_regret + EPSILON) / (first_regret + second_regret + 2.0 * EPSILON)


def order_floats(key):
    centred = key - (1 << 29)
    size = jnp.where(centred >= 0, centred, -1 - centred)
    power = size >> 23
    value = ((size & ((1 << 23) - 1)) + (1 << 23)).astype(jnp.float32)
    for bit in range(6):
        value = value * jnp.where((power >> bit) & 1 == 1, float(2 ** (2**bit)), 1.0)
    return jnp.where(centred >= 0, value, -value)


ROOT_CHECK, ROOT_BET, FC_FOLD, FC_CALL, AC_CHECK, AC_BET, FB_FOLD, FB_CALL = range(8)


def reaches(regrets, one_range, range_two, live):
    share_root = action_share(regrets[ROOT_CHECK], regrets[ROOT_BET])
    share_fc = action_share(regrets[FC_FOLD], regrets[FC_CALL])
    share_ac = action_share(regrets[AC_CHECK], regrets[AC_BET])
    share_fb = action_share(regrets[FB_FOLD], regrets[FB_CALL])
    one_all = one_range * live
    one_check = one_all * share_root
    one_cbf = one_check * share_fc
    two_all = range_two * live
    two_cc = two_all * share_ac
    two_bf = two_all * share_fb
    shares = (share_root, share_fc, share_ac, share_fb)
    return shares, (two_all, two_cc, two_bf, one_all, one_check, one_cbf)


def turn_rows(cols):
    two_all, two_cc, two_bf, one_all, one_check, one_cbf = cols
    return (
        one_check,
        one_all - one_check,
        one_check - one_cbf,
        two_cc,
        two_all - two_bf,
        two_all - two_cc,
    )


def step_kernel(
    step,
    compat_ref,
    order_ref,
    live_ref,
    alive_ref,
    share_ref,
    one_ref,
    two_ref,
    *rest,
):
    if step == 0:
        regret_out, turn_out, cont_ref, minus_ref, cols_ref, sign_ref, weight_ref = rest
        regrets = [jnp.zeros(live_ref.shape, jnp.float32)] * 8
    else:
        (
            regret_in,
            turn_in,
            regret_out,
            turn_out,
            cont_ref,
            minus_ref,
            cols_ref,
            sign_ref,
            weight_ref,
        ) = rest
        regrets = [regret_in[row] for row in range(8)]
    slots, width = live_ref.shape
    live = live_ref[...]
    alive = alive_ref[...]
    shares, cols = reaches(regrets, one_ref[...], two_ref[...], live)
    iter_weight = float(step + 1)
    for row, term in enumerate(turn_rows(cols)):
        if step == 0:
            turn_out[row] = iter_weight * term
        else:
            turn_out[row] = turn_in[row] + iter_weight * term
    for row in range(6):
        cols_ref[:, row, :] = cols[row].astype(jnp.bfloat16).astype(jnp.float32) * alive
    for row in range(6, 8):
        cols_ref[:, row, :] = jnp.zeros_like(alive)
    minus_ref[...] = -compat_ref[...]

    def one_flop(slot, carry):
        mine = order_ref[pl.ds(slot, 1), :]
        cols_now = cols_ref[slot].astype(jnp.bfloat16)
        total = jnp.zeros((8, width), jnp.float32)
        for first in range(0, width, BLOCK):
            last = min(first + BLOCK, width)
            theirs = jnp.concatenate(
                [
                    jnp.transpose(jnp.broadcast_to(mine[:, spot : spot + 128], (128, 128)))
                    for spot in range(first, last, 128)
                ],
                axis=0,
            )
            blocks = []
            for spot in range(0, width, 128):
                gap = (mine[:, spot : spot + 128] - theirs).astype(jnp.bfloat16)
                limit = compat_ref[first:last, spot : spot + 128]
                blocks.append(
                    jnp.minimum(
                        jnp.maximum(gap, minus_ref[first:last, spot : spot + 128]), limit
                    )
                )
            sign_block = jnp.concatenate(blocks, axis=1)
            total = total + jnp.dot(
                cols_now[:, first:last], sign_block, preferred_element_type=jnp.float32
            )
        sign_ref[slot] = total
        return carry

    lax.fori_loop(0, slots, one_flop, 0)
    all_cols = cols_ref[...].reshape(slots * 8, width).astype(jnp.bfloat16)
    weight_ref[...] = jnp.dot(
        all_cols, compat_ref[...], preferred_element_type=jnp.float32
    ).reshape(slots, 8, width)

    share_root, share_fc, share_ac, share_fb = shares
    scale = 1.0 / HANDS
    sv = [sign_ref[:, row, :] * alive for row in range(6)]
    wv = [weight_ref[:, row, :] * alive for row in range(6)]
    v_cc = 0.5 * scale * sv[1]
    v_cbf = -0.5 * scale * (wv[0] - wv[1])
    v_cbc = 1.5 * scale * (sv[0] - sv[1])
    v_bf = 0.5 * scale * wv[2]
    v_bc = 1.5 * scale * (sv[0] - sv[2])
    w_cc = 0.5 * scale * sv[4]
    w_cbf = 0.5 * scale * wv[5]
    w_cbc = 1.5 * scale * (sv[4] - sv[5])
    w_bf = -0.5 * scale * (wv[3] - wv[4])
    w_bc = 1.5 * scale * (sv[3] - sv[4])
    u_fc = share_fc * v_cbf + (1.0 - share_fc) * v_cbc
    v_check = v_cc + u_fc
    v_bet = v_bf + v_bc
    u_root = share_root * v_check + (1.0 - share_root) * v_bet
    x_bet = w_cbf + w_cbc
    u_ac = share_ac * w_cc + (1.0 - share_ac) * x_bet
    u_fb = share_fb * w_bf + (1.0 - share_fb) * w_bc
    updates = (
        (ROOT_CHECK, v_check, u_root),
        (ROOT_BET, v_bet, u_root),
        (FC_FOLD, v_cbf, u_fc),
        (FC_CALL, v_cbc, u_fc),
        (AC_CHECK, w_cc, u_ac),
        (AC_BET, x_bet, u_ac),
        (FB_FOLD, w_bf, u_fb),
        (FB_CALL, w_bc, u_fb),
    )
    for row, value, node in updates:
        regret_out[row] = jnp.maximum(regrets[row] + value - node, 0.0)
    cont_ref[...] = jnp.sum(share_ref[...] * u_root, axis=0, keepdims=True)


def run_step(step, *operands):
    slots, width = operands[1].shape
    vmem = pl.BlockSpec(memory_space=pltpu.VMEM)
    return pl.pallas_call(
        functools.partial(step_kernel, step),
        out_shape=(
            jax.ShapeDtypeStruct((8, slots, width), jnp.float32),
            jax.ShapeDtypeStruct((6, slots, width), jnp.float32),
            jax.ShapeDtypeStruct((1, width), jnp.float32),
        ),
        in_specs=[vmem] * len(operands),
        out_specs=(vmem,) * 3,
        scratch_shapes=[
            pltpu.VMEM((width, width), jnp.bfloat16),
            pltpu.VMEM((slots, 8, width), jnp.float32),
            pltpu.VMEM((slots, 8, width), jnp.float32),
            pltpu.VMEM((slots, 8, width), jnp.float32),
        ],
        compiler_params=pltpu.CompilerParams(vmem_limit_bytes=56 * 1024 * 1024),
    )(*operands)


def sum_kernel(
    groups, shards, part_ref, out_ref, first, middle, second, sent1, came1, sent2, came2
):
    spots = (("inf", lax.axis_index("inf"), shards), ("grp", lax.axis_index("grp"), groups))
    barrier = pltpu.get_barrier_semaphore()
    for axis, spot, size in spots:
        for hop in range(1, size):
            pl.semaphore_signal(
                barrier,
                inc=1,
                device_id={axis: lax.rem(spot + hop, size)},
                device_id_type=pl.DeviceIdType.MESH,
            )
    pl.semaphore_wait(barrier, groups + shards - 2)

    def exchange(axis, spot, size, source, slots, sent, came):
        def move(hop, slot, target):
            return pltpu.make_async_remote_copy(
                src_ref=source,
                dst_ref=slots.at[slot],
                send_sem=sent.at[hop],
                recv_sem=came.at[slot],
                device_id={axis: target},
                device_id_type=pl.DeviceIdType.MESH,
            )

        for hop in range(1, size):
            move(hop, spot, lax.rem(spot + hop, size)).start()
        slots[spot] = source[...]
        for hop in range(1, size):
            sender = lax.rem(spot + size - hop, size)
            move(hop, sender, sender).wait_recv()
        total = slots[0]
        for slot in range(1, size):
            total = total + slots[slot]
        for hop in range(1, size):
            move(hop, spot, lax.rem(spot + hop, size)).wait_send()
        return total

    middle[...] = exchange(*spots[0], part_ref, first, sent1, came1)
    out_ref[...] = exchange(*spots[1], middle, second, sent2, came2)


def sum_all(part, groups, shards):
    vmem = pl.BlockSpec(memory_space=pltpu.VMEM)
    return pl.pallas_call(
        functools.partial(sum_kernel, groups, shards),
        out_shape=jax.ShapeDtypeStruct(part.shape, part.dtype),
        in_specs=[vmem],
        out_specs=vmem,
        scratch_shapes=[
            pltpu.VMEM((shards,) + part.shape, part.dtype),
            pltpu.VMEM(part.shape, part.dtype),
            pltpu.VMEM((groups,) + part.shape, part.dtype),
            pltpu.SemaphoreType.DMA((shards,)),
            pltpu.SemaphoreType.DMA((shards,)),
            pltpu.SemaphoreType.DMA((groups,)),
            pltpu.SemaphoreType.DMA((groups,)),
        ],
        compiler_params=pltpu.CompilerParams(collective_id=0, has_side_effects=True),
    )(part)


def last_kernel(total_weight, live_ref, one_ref, two_ref, regret_ref, turn_ref, out_ref):
    regrets = [regret_ref[row] for row in range(8)]
    unused, cols = reaches(regrets, one_ref[...], two_ref[...], live_ref[...])
    for row, term in enumerate(turn_rows(cols)):
        out_ref[row] = (turn_ref[row] + float(ITERS) * term) / total_weight


def on_device(range_one, range_two, flop_weight, board_mask, runout, strength):
    groups = lax.axis_size("grp")
    shards = lax.axis_size("inf")
    shard_id = lax.axis_index("inf")
    group_id = lax.axis_index("grp")
    low_table, high_table = hand_cards(H, HANDS)
    low_all = jnp.asarray(low_table)
    high_all = jnp.asarray(high_table)
    capacity = strength.shape[0]
    hand_block = strength.shape[2]
    flop_total = 12.0 * FLOP_GRP * groups
    rounds = ITERS - 1
    local_count = FLOP_GRP // shards

    small = jnp.concatenate(
        [flop_weight[:, None], runout[:, :rounds].reshape(capacity, 2 * rounds)], axis=1
    )
    small_all = lax.all_gather(small, "grp", axis=0, tiled=False)
    counts = jnp.sum((small_all[:, :, 0] > 0).astype(jnp.int32), axis=1, dtype=jnp.int32)
    rows = jnp.arange(capacity)
    group_ids = jnp.arange(groups)
    earlier = (group_ids[None, :] < group_ids[:, None]).astype(jnp.int32)
    place = jnp.sum(
        jnp.minimum(counts[None, None, :], rows[None, :, None] + earlier[:, None, :]),
        axis=2,
        dtype=jnp.int32,
    )
    place = jnp.where(rows[None, :] < counts[:, None], place, -1)

    masked = jnp.where(board_mask[:, None, :] == 1, strength[:, :rounds], -1)
    masked = masked.reshape(capacity, rounds * hand_block)
    own_place = jnp.sum(
        jnp.where(group_ids[:, None] == group_id, place, 0), axis=0, dtype=jnp.int32
    )
    target = jnp.arange(groups * FLOP_GRP)
    match = own_place[None, :] == target[:, None]
    is_valid = jnp.any(match, axis=1)
    source = jnp.sum(jnp.where(match, rows[None, :], 0), axis=1, dtype=jnp.int32)
    taken = jnp.where(is_valid[:, None], jnp.take(masked, source, axis=0), 0)
    arrived = lax.all_to_all(
        taken.reshape(groups, FLOP_GRP, rounds * hand_block),
        "grp",
        split_axis=0,
        concat_axis=0,
        tiled=True,
    )
    key_rows = jnp.sum(arrived, axis=0, dtype=jnp.int32).reshape(FLOP_GRP, rounds, hand_block)
    flop_keys = lax.all_to_all(key_rows, "inf", split_axis=0, concat_axis=2, tiled=True)

    here = group_id * FLOP_GRP + shard_id * local_count + jnp.arange(local_count)
    mine = place.reshape(1, -1) == here[:, None]
    small_here = jnp.sum(
        jnp.where(mine[:, :, None], small_all.reshape(1, groups * capacity, -1), 0),
        axis=1,
        dtype=jnp.int32,
    )
    flop_share = small_here[:, 0:1].astype(jnp.float32) / flop_total

    is_hand = (jnp.arange(H) < HANDS)[None, :]
    is_live = (flop_keys[:, 0, :] >= 0) & is_hand
    live = is_live.astype(jnp.float32)
    compat = (low_all[:, None] != low_all[None, :]) & (low_all[:, None] != high_all[None, :])
    compat = compat & (high_all[:, None] != low_all[None, :])
    compat = compat & (high_all[:, None] != high_all[None, :])
    compat = compat.astype(jnp.bfloat16)

    two_row = range_two[None, :]
    pre_fold = jnp.zeros((1, H), jnp.float32)
    pre_cont = jnp.zeros((1, H), jnp.float32)
    pre_sum = jnp.zeros((1, H), jnp.float32)
    state = ()
    for step in range(rounds):
        share_pre = action_share(pre_cont, pre_fold)
        one_range = range_one[None, :] * share_pre
        turn_card = small_here[:, 1 + 2 * step : 2 + 2 * step]
        river_card = small_here[:, 2 + 2 * step : 3 + 2 * step]
        blocked = (low_all[None, :] == turn_card) | (low_all[None, :] == river_card)
        blocked = blocked | (high_all[None, :] == turn_card) | (high_all[None, :] == river_card)
        alive = (is_live & jnp.logical_not(blocked)).astype(jnp.float32)
        regrets, turn_sum, cont_part = run_step(
            step,
            compat,
            order_floats(jnp.maximum(flop_keys[:, step, :], 0)),
            live,
            alive,
            flop_share,
            one_range,
            two_row,
            *state,
        )
        state = (regrets, turn_sum)
        cont_value = sum_all(cont_part, groups, shards)
        u_pre = share_pre * cont_value + (1.0 - share_pre) * FOLD_VALUE
        pre_cont = jnp.maximum(pre_cont + cont_value - u_pre, 0.0)
        pre_fold = jnp.maximum(pre_fold + FOLD_VALUE - u_pre, 0.0)
        pre_sum = pre_sum + float(step + 1) * one_range
    total_weight = ITERS * (ITERS + 1) / 2.0
    one_range = range_one[None, :] * action_share(pre_cont, pre_fold)
    turn_final = pl.pallas_call(
        functools.partial(last_kernel, total_weight),
        out_shape=jax.ShapeDtypeStruct((6, local_count, H), jnp.float32),
        in_specs=[pl.BlockSpec(memory_space=pltpu.VMEM)] * 5,
        out_specs=pl.BlockSpec(memory_space=pltpu.VMEM),
    )(live, one_range, two_row, *state)
    turn_final = jnp.transpose(turn_final, (1, 0, 2))
    pre_sum = (pre_sum + float(ITERS) * one_range) / total_weight
    pre_block = lax.dynamic_slice_in_dim(pre_sum[0], shard_id * hand_block, hand_block)
    return (turn_final, pre_block)


def solution(mesh):
    in_specs = (P(), P(), P("grp"), P("grp", "inf"), P("grp", None, None), P("grp", None, "inf"))
    out_specs = (P(("grp", "inf"), None, None), P("inf"))
    return jax.shard_map(
        on_device, mesh=mesh, in_specs=in_specs, out_specs=out_specs, check_vma=False
    )
```

```python
import functools

import jax
import jax.numpy as jnp
import numpy as np
from jax import lax
from jax.experimental import pallas as pl
from jax.experimental.pallas import tpu as pltpu
from jax.sharding import PartitionSpec as P

HANDS = 1326
H = 1408
ITERS = 4
FLOP_GRP = 128


EPSILON = 0.01
FOLD_VALUE = -0.1
BLOCK = 256


def hand_cards(slot_total, real_total):
    low_list = []
    high_list = []
    for first_card in range(52):
        for second_card in range(first_card + 1, 52):
            low_list.append(first_card)
            high_list.append(second_card)
    low_table = np.full(slot_total, 52, np.int32)
    high_table = np.full(slot_total, 53, np.int32)
    used_count = min(slot_total, real_total)
    low_table[:used_count] = np.array(low_list[:used_count], np.int32)
    high_table[:used_count] = np.array(high_list[:used_count], np.int32)
    return (low_table, high_table)


def action_share(first_regret, second_regret):
    return (first_regret + EPSILON) / (first_regret + second_regret + 2.0 * EPSILON)


def order_floats(key):
    centred = key - (1 << 29)
    size = jnp.where(centred >= 0, centred, -1 - centred)
    power = size >> 23
    value = ((size & ((1 << 23) - 1)) + (1 << 23)).astype(jnp.float32)
    for bit in range(6):
        value = value * jnp.where((power >> bit) & 1 == 1, float(2 ** (2**bit)), 1.0)
    return jnp.where(centred >= 0, value, -value)


ROOT_CHECK, ROOT_BET, FC_FOLD, FC_CALL, AC_CHECK, AC_BET, FB_FOLD, FB_CALL = range(8)


def reaches(regrets, one_range, range_two, live):
    share_root = action_share(regrets[ROOT_CHECK], regrets[ROOT_BET])
    share_fc = action_share(regrets[FC_FOLD], regrets[FC_CALL])
    share_ac = action_share(regrets[AC_CHECK], regrets[AC_BET])
    share_fb = action_share(regrets[FB_FOLD], regrets[FB_CALL])
    one_all = one_range * live
    one_check = one_all * share_root
    one_cbf = one_check * share_fc
    two_all = range_two * live
    two_cc = two_all * share_ac
    two_bf = two_all * share_fb
    shares = (share_root, share_fc, share_ac, share_fb)
    return shares, (two_all, two_cc, two_bf, one_all, one_check, one_cbf)


def turn_rows(cols):
    two_all, two_cc, two_bf, one_all, one_check, one_cbf = cols
    return (
        one_check,
        one_all - one_check,
        one_check - one_cbf,
        two_cc,
        two_all - two_bf,
        two_all - two_cc,
    )


def step_kernel(
    step,
    compat_ref,
    order_ref,
    live_ref,
    alive_ref,
    share_ref,
    one_ref,
    two_ref,
    *rest,
):
    if step == 0:
        regret_out, turn_out, cont_ref, minus_ref, cols_ref, sign_ref, weight_ref = rest
        regrets = [jnp.zeros(live_ref.shape, jnp.float32)] * 8
    else:
        (
            regret_in,
            turn_in,
            regret_out,
            turn_out,
            cont_ref,
            minus_ref,
            cols_ref,
            sign_ref,
            weight_ref,
        ) = rest
        regrets = [regret_in[row] for row in range(8)]
    slots, width = live_ref.shape
    live = live_ref[...]
    alive = alive_ref[...]
    shares, cols = reaches(regrets, one_ref[...], two_ref[...], live)
    iter_weight = float(step + 1)
    for row, term in enumerate(turn_rows(cols)):
        if step == 0:
            turn_out[row] = iter_weight * term
        else:
            turn_out[row] = turn_in[row] + iter_weight * term
    for row in range(6):
        cols_ref[:, row, :] = cols[row].astype(jnp.bfloat16).astype(jnp.float32) * alive
    for row in range(6, 8):
        cols_ref[:, row, :] = jnp.zeros_like(alive)
    minus_ref[...] = -compat_ref[...]

    def one_flop(slot, carry):
        mine = order_ref[pl.ds(slot, 1), :]
        cols_now = cols_ref[slot].astype(jnp.bfloat16)
        total = jnp.zeros((8, width), jnp.float32)
        for first in range(0, width, BLOCK):
            last = min(first + BLOCK, width)
            theirs = jnp.concatenate(
                [
                    jnp.transpose(jnp.broadcast_to(mine[:, spot : spot + 128], (128, 128)))
                    for spot in range(first, last, 128)
                ],
                axis=0,
            )
            blocks = []
            for spot in range(0, width, 128):
                gap = (mine[:, spot : spot + 128] - theirs).astype(jnp.bfloat16)
                limit = compat_ref[first:last, spot : spot + 128]
                blocks.append(
                    jnp.minimum(
                        jnp.maximum(gap, minus_ref[first:last, spot : spot + 128]), limit
                    )
                )
            sign_block = jnp.concatenate(blocks, axis=1)
            total = total + jnp.dot(
                cols_now[:, first:last], sign_block, preferred_element_type=jnp.float32
            )
        sign_ref[slot] = total
        return carry

    lax.fori_loop(0, slots, one_flop, 0)
    all_cols = cols_ref[...].reshape(slots * 8, width).astype(jnp.bfloat16)
    weight_ref[...] = jnp.dot(
        all_cols, compat_ref[...], preferred_element_type=jnp.float32
    ).reshape(slots, 8, width)

    share_root, share_fc, share_ac, share_fb = shares
    scale = 1.0 / HANDS
    sv = [sign_ref[:, row, :] * alive for row in range(6)]
    wv = [weight_ref[:, row, :] * alive for row in range(6)]
    v_cc = 0.5 * scale * sv[1]
    v_cbf = -0.5 * scale * (wv[0] - wv[1])
    v_cbc = 1.5 * scale * (sv[0] - sv[1])
    v_bf = 0.5 * scale * wv[2]
    v_bc = 1.5 * scale * (sv[0] - sv[2])
    w_cc = 0.5 * scale * sv[4]
    w_cbf = 0.5 * scale * wv[5]
    w_cbc = 1.5 * scale * (sv[4] - sv[5])
    w_bf = -0.5 * scale * (wv[3] - wv[4])
    w_bc = 1.5 * scale * (sv[3] - sv[4])
    u_fc = share_fc * v_cbf + (1.0 - share_fc) * v_cbc
    v_check = v_cc + u_fc
    v_bet = v_bf + v_bc
    u_root = share_root * v_check + (1.0 - share_root) * v_bet
    x_bet = w_cbf + w_cbc
    u_ac = share_ac * w_cc + (1.0 - share_ac) * x_bet
    u_fb = share_fb * w_bf + (1.0 - share_fb) * w_bc
    updates = (
        (ROOT_CHECK, v_check, u_root),
        (ROOT_BET, v_bet, u_root),
        (FC_FOLD, v_cbf, u_fc),
        (FC_CALL, v_cbc, u_fc),
        (AC_CHECK, w_cc, u_ac),
        (AC_BET, x_bet, u_ac),
        (FB_FOLD, w_bf, u_fb),
        (FB_CALL, w_bc, u_fb),
    )
    for row, value, node in updates:
        regret_out[row] = jnp.maximum(regrets[row] + value - node, 0.0)
    cont_ref[...] = jnp.sum(share_ref[...] * u_root, axis=0, keepdims=True)


def run_step(step, *operands):
    slots, width = operands[1].shape
    vmem = pl.BlockSpec(memory_space=pltpu.VMEM)
    return pl.pallas_call(
        functools.partial(step_kernel, step),
        out_shape=(
            jax.ShapeDtypeStruct((8, slots, width), jnp.float32),
            jax.ShapeDtypeStruct((6, slots, width), jnp.float32),
            jax.ShapeDtypeStruct((1, width), jnp.float32),
        ),
        in_specs=[vmem] * len(operands),
        out_specs=(vmem,) * 3,
        scratch_shapes=[
            pltpu.VMEM((width, width), jnp.bfloat16),
            pltpu.VMEM((slots, 8, width), jnp.float32),
            pltpu.VMEM((slots, 8, width), jnp.float32),
            pltpu.VMEM((slots, 8, width), jnp.float32),
        ],
        compiler_params=pltpu.CompilerParams(vmem_limit_bytes=56 * 1024 * 1024),
        cost_estimate=pl.CostEstimate(
            flops=16 * slots * width * width,
            bytes_accessed=2 * slots * width * width,
            transcendentals=0,
        ),
    )(*operands)


def sum_kernel(
    groups, shards, part_ref, out_ref, first, middle, second, sent1, came1, sent2, came2
):
    spots = (("inf", lax.axis_index("inf"), shards), ("grp", lax.axis_index("grp"), groups))
    barrier = pltpu.get_barrier_semaphore()
    for axis, spot, size in spots:
        for hop in range(1, size):
            pl.semaphore_signal(
                barrier,
                inc=1,
                device_id={axis: lax.rem(spot + hop, size)},
                device_id_type=pl.DeviceIdType.MESH,
            )
    pl.semaphore_wait(barrier, groups + shards - 2)

    def exchange(axis, spot, size, source, slots, sent, came):
        def move(hop, slot, target):
            return pltpu.make_async_remote_copy(
                src_ref=source,
                dst_ref=slots.at[slot],
                send_sem=sent.at[hop],
                recv_sem=came.at[slot],
                device_id={axis: target},
                device_id_type=pl.DeviceIdType.MESH,
            )

        for hop in range(1, size):
            move(hop, spot, lax.rem(spot + hop, size)).start()
        slots[spot] = source[...]
        for hop in range(1, size):
            sender = lax.rem(spot + size - hop, size)
            move(hop, sender, sender).wait_recv()
        total = slots[0]
        for slot in range(1, size):
            total = total + slots[slot]
        for hop in range(1, size):
            move(hop, spot, lax.rem(spot + hop, size)).wait_send()
        return total

    middle[...] = exchange(*spots[0], part_ref, first, sent1, came1)
    out_ref[...] = exchange(*spots[1], middle, second, sent2, came2)


def sum_all(part, groups, shards):
    vmem = pl.BlockSpec(memory_space=pltpu.VMEM)
    return pl.pallas_call(
        functools.partial(sum_kernel, groups, shards),
        out_shape=jax.ShapeDtypeStruct(part.shape, part.dtype),
        in_specs=[vmem],
        out_specs=vmem,
        scratch_shapes=[
            pltpu.VMEM((shards,) + part.shape, part.dtype),
            pltpu.VMEM(part.shape, part.dtype),
            pltpu.VMEM((groups,) + part.shape, part.dtype),
            pltpu.SemaphoreType.DMA((shards,)),
            pltpu.SemaphoreType.DMA((shards,)),
            pltpu.SemaphoreType.DMA((groups,)),
            pltpu.SemaphoreType.DMA((groups,)),
        ],
        compiler_params=pltpu.CompilerParams(collective_id=0, has_side_effects=True),
        cost_estimate=pl.CostEstimate(flops=0, bytes_accessed=30_000_000, transcendentals=0),
    )(part)


def last_kernel(total_weight, live_ref, one_ref, two_ref, regret_ref, turn_ref, out_ref):
    regrets = [regret_ref[row] for row in range(8)]
    unused, cols = reaches(regrets, one_ref[...], two_ref[...], live_ref[...])
    for row, term in enumerate(turn_rows(cols)):
        out_ref[row] = (turn_ref[row] + float(ITERS) * term) / total_weight


def on_device(range_one, range_two, flop_weight, board_mask, runout, strength):
    groups = lax.axis_size("grp")
    shards = lax.axis_size("inf")
    shard_id = lax.axis_index("inf")
    group_id = lax.axis_index("grp")
    low_table, high_table = hand_cards(H, HANDS)
    low_all = jnp.asarray(low_table)
    high_all = jnp.asarray(high_table)
    capacity = strength.shape[0]
    hand_block = strength.shape[2]
    flop_total = 12.0 * FLOP_GRP * groups
    rounds = ITERS - 1
    local_count = FLOP_GRP // shards

    small = jnp.concatenate(
        [flop_weight[:, None], runout[:, :rounds].reshape(capacity, 2 * rounds)], axis=1
    )
    small_all = lax.all_gather(small, "grp", axis=0, tiled=False)
    counts = jnp.sum((small_all[:, :, 0] > 0).astype(jnp.int32), axis=1, dtype=jnp.int32)
    rows = jnp.arange(capacity)
    group_ids = jnp.arange(groups)
    earlier = (group_ids[None, :] < group_ids[:, None]).astype(jnp.int32)
    place = jnp.sum(
        jnp.minimum(counts[None, None, :], rows[None, :, None] + earlier[:, None, :]),
        axis=2,
        dtype=jnp.int32,
    )
    place = jnp.where(rows[None, :] < counts[:, None], place, -1)

    own_place = jnp.sum(
        jnp.where(group_ids[:, None] == group_id, place, 0), axis=0, dtype=jnp.int32
    )
    target = jnp.arange(groups * FLOP_GRP)
    match = own_place[None, :] == target[:, None]
    is_valid = jnp.any(match, axis=1)
    source = jnp.sum(jnp.where(match, rows[None, :], 0), axis=1, dtype=jnp.int32)

    def send_keys(first, last):
        span = last - first
        masked = jnp.where(board_mask[:, None, :] == 1, strength[:, first:last], -1)
        masked = masked.reshape(capacity, span * hand_block)
        taken = jnp.where(is_valid[:, None], jnp.take(masked, source, axis=0), 0)
        arrived = lax.all_to_all(
            taken.reshape(groups, FLOP_GRP, span * hand_block),
            "grp",
            split_axis=0,
            concat_axis=0,
            tiled=True,
        )
        key_rows = jnp.sum(arrived, axis=0, dtype=jnp.int32).reshape(
            shards, local_count, span, hand_block
        )
        wholes = []
        for spot in range(span):
            whole = lax.all_to_all(
                key_rows[:, :, spot, :], "inf", split_axis=0, concat_axis=0, tiled=True
            )
            wholes.append(jnp.transpose(whole, (1, 0, 2)).reshape(local_count, H))
        return wholes

    flop_keys = send_keys(0, 1) + send_keys(1, rounds)

    here = group_id * FLOP_GRP + shard_id * local_count + jnp.arange(local_count)
    mine = place.reshape(1, -1) == here[:, None]
    small_here = jnp.sum(
        jnp.where(mine[:, :, None], small_all.reshape(1, groups * capacity, -1), 0),
        axis=1,
        dtype=jnp.int32,
    )
    flop_share = small_here[:, 0:1].astype(jnp.float32) / flop_total

    is_hand = (jnp.arange(H) < HANDS)[None, :]
    is_live = (flop_keys[0] >= 0) & is_hand
    live = is_live.astype(jnp.float32)
    compat = (low_all[:, None] != low_all[None, :]) & (low_all[:, None] != high_all[None, :])
    compat = compat & (high_all[:, None] != low_all[None, :])
    compat = compat & (high_all[:, None] != high_all[None, :])
    compat = compat.astype(jnp.bfloat16)

    two_row = range_two[None, :]
    pre_fold = jnp.zeros((1, H), jnp.float32)
    pre_cont = jnp.zeros((1, H), jnp.float32)
    pre_sum = jnp.zeros((1, H), jnp.float32)
    state = ()
    for step in range(rounds):
        share_pre = action_share(pre_cont, pre_fold)
        one_range = range_one[None, :] * share_pre
        turn_card = small_here[:, 1 + 2 * step : 2 + 2 * step]
        river_card = small_here[:, 2 + 2 * step : 3 + 2 * step]
        blocked = (low_all[None, :] == turn_card) | (low_all[None, :] == river_card)
        blocked = blocked | (high_all[None, :] == turn_card) | (high_all[None, :] == river_card)
        alive = (is_live & jnp.logical_not(blocked)).astype(jnp.float32)
        regrets, turn_sum, cont_part = run_step(
            step,
            compat,
            order_floats(jnp.maximum(flop_keys[step], 0)),
            live,
            alive,
            flop_share,
            one_range,
            two_row,
            *state,
        )
        state = (regrets, turn_sum)
        cont_value = sum_all(cont_part, groups, shards)
        u_pre = share_pre * cont_value + (1.0 - share_pre) * FOLD_VALUE
        pre_cont = jnp.maximum(pre_cont + cont_value - u_pre, 0.0)
        pre_fold = jnp.maximum(pre_fold + FOLD_VALUE - u_pre, 0.0)
        pre_sum = pre_sum + float(step + 1) * one_range
    total_weight = ITERS * (ITERS + 1) / 2.0
    one_range = range_one[None, :] * action_share(pre_cont, pre_fold)
    turn_final = pl.pallas_call(
        functools.partial(last_kernel, total_weight),
        out_shape=jax.ShapeDtypeStruct((6, local_count, H), jnp.float32),
        in_specs=[pl.BlockSpec(memory_space=pltpu.VMEM)] * 5,
        out_specs=pl.BlockSpec(memory_space=pltpu.VMEM),
    )(live, one_range, two_row, *state)
    turn_final = jnp.transpose(turn_final, (1, 0, 2))
    pre_sum = (pre_sum + float(ITERS) * one_range) / total_weight
    pre_block = lax.dynamic_slice_in_dim(pre_sum[0], shard_id * hand_block, hand_block)
    return (turn_final, pre_block)


def solution(mesh):
    in_specs = (P(), P(), P("grp"), P("grp", "inf"), P("grp", None, None), P("grp", None, "inf"))
    out_specs = (P(("grp", "inf"), None, None), P("inf"))
    return jax.shard_map(
        on_device, mesh=mesh, in_specs=in_specs, out_specs=out_specs, check_vma=False
    )
```

```python
import functools

import jax
import jax.numpy as jnp
import numpy as np
from jax import lax
from jax.experimental import pallas as pl
from jax.experimental.pallas import tpu as pltpu
from jax.sharding import PartitionSpec as P

HANDS = 1326
H = 1408
ITERS = 4
FLOP_GRP = 128


EPSILON = 0.01
FOLD_VALUE = -0.1
BLOCK = 256


def hand_cards(slot_total, real_total):
    low_list = []
    high_list = []
    for first_card in range(52):
        for second_card in range(first_card + 1, 52):
            low_list.append(first_card)
            high_list.append(second_card)
    low_table = np.full(slot_total, 52, np.int32)
    high_table = np.full(slot_total, 53, np.int32)
    used_count = min(slot_total, real_total)
    low_table[:used_count] = np.array(low_list[:used_count], np.int32)
    high_table[:used_count] = np.array(high_list[:used_count], np.int32)
    return (low_table, high_table)


def action_share(first_regret, second_regret):
    return (first_regret + EPSILON) / (first_regret + second_regret + 2.0 * EPSILON)


def order_floats(key):
    centred = key - (1 << 29)
    size = jnp.where(centred >= 0, centred, -1 - centred)
    power = size >> 23
    value = ((size & ((1 << 23) - 1)) + (1 << 23)).astype(jnp.float32)
    for bit in range(6):
        value = value * jnp.where((power >> bit) & 1 == 1, float(2 ** (2**bit)), 1.0)
    return jnp.where(centred >= 0, value, -value)


ROOT_CHECK, ROOT_BET, FC_FOLD, FC_CALL, AC_CHECK, AC_BET, FB_FOLD, FB_CALL = range(8)


def reaches(regrets, one_range, range_two, live):
    share_root = action_share(regrets[ROOT_CHECK], regrets[ROOT_BET])
    share_fc = action_share(regrets[FC_FOLD], regrets[FC_CALL])
    share_ac = action_share(regrets[AC_CHECK], regrets[AC_BET])
    share_fb = action_share(regrets[FB_FOLD], regrets[FB_CALL])
    one_all = one_range * live
    one_check = one_all * share_root
    one_cbf = one_check * share_fc
    two_all = range_two * live
    two_cc = two_all * share_ac
    two_bf = two_all * share_fb
    shares = (share_root, share_fc, share_ac, share_fb)
    return shares, (two_all, two_cc, two_bf, one_all, one_check, one_cbf)


def turn_rows(cols):
    two_all, two_cc, two_bf, one_all, one_check, one_cbf = cols
    return (
        one_check,
        one_all - one_check,
        one_check - one_cbf,
        two_cc,
        two_all - two_bf,
        two_all - two_cc,
    )


def step_kernel(
    step,
    compat_ref,
    order_ref,
    live_ref,
    alive_ref,
    share_ref,
    one_ref,
    two_ref,
    *rest,
):
    if step == 0:
        regret_out, turn_out, cont_ref, minus_ref, cols_ref, sign_ref, weight_ref = rest
        regrets = [jnp.zeros(live_ref.shape, jnp.float32)] * 8
    else:
        (
            regret_in,
            turn_in,
            regret_out,
            turn_out,
            cont_ref,
            minus_ref,
            cols_ref,
            sign_ref,
            weight_ref,
        ) = rest
        regrets = [regret_in[row] for row in range(8)]
    slots, width = live_ref.shape
    live = live_ref[...]
    alive = alive_ref[...]
    shares, cols = reaches(regrets, one_ref[...], two_ref[...], live)
    iter_weight = float(step + 1)
    for row, term in enumerate(turn_rows(cols)):
        if step == 0:
            turn_out[row] = iter_weight * term
        else:
            turn_out[row] = turn_in[row] + iter_weight * term
    for row in range(6):
        cols_ref[:, row, :] = cols[row].astype(jnp.bfloat16).astype(jnp.float32) * alive
    for row in range(6, 8):
        cols_ref[:, row, :] = jnp.zeros_like(alive)
    minus_ref[...] = -compat_ref[...]

    def one_flop(slot, carry):
        mine = order_ref[pl.ds(slot, 1), :]
        cols_now = cols_ref[slot].astype(jnp.bfloat16)
        total = jnp.zeros((8, width), jnp.float32)
        for first in range(0, width, BLOCK):
            last = min(first + BLOCK, width)
            theirs = jnp.concatenate(
                [
                    jnp.transpose(jnp.broadcast_to(mine[:, spot : spot + 128], (128, 128)))
                    for spot in range(first, last, 128)
                ],
                axis=0,
            )
            blocks = []
            for spot in range(0, width, 128):
                gap = (mine[:, spot : spot + 128] - theirs).astype(jnp.bfloat16)
                limit = compat_ref[first:last, spot : spot + 128]
                blocks.append(
                    jnp.minimum(
                        jnp.maximum(gap, minus_ref[first:last, spot : spot + 128]), limit
                    )
                )
            sign_block = jnp.concatenate(blocks, axis=1)
            total = total + jnp.dot(
                cols_now[:, first:last], sign_block, preferred_element_type=jnp.float32
            )
        sign_ref[slot] = total
        return carry

    lax.fori_loop(0, slots, one_flop, 0)
    all_cols = cols_ref[...].reshape(slots * 8, width).astype(jnp.bfloat16)
    weight_ref[...] = jnp.dot(
        all_cols, compat_ref[...], preferred_element_type=jnp.float32
    ).reshape(slots, 8, width)

    share_root, share_fc, share_ac, share_fb = shares
    scale = 1.0 / HANDS
    sv = [sign_ref[:, row, :] * alive for row in range(6)]
    wv = [weight_ref[:, row, :] * alive for row in range(6)]
    v_cc = 0.5 * scale * sv[1]
    v_cbf = -0.5 * scale * (wv[0] - wv[1])
    v_cbc = 1.5 * scale * (sv[0] - sv[1])
    v_bf = 0.5 * scale * wv[2]
    v_bc = 1.5 * scale * (sv[0] - sv[2])
    w_cc = 0.5 * scale * sv[4]
    w_cbf = 0.5 * scale * wv[5]
    w_cbc = 1.5 * scale * (sv[4] - sv[5])
    w_bf = -0.5 * scale * (wv[3] - wv[4])
    w_bc = 1.5 * scale * (sv[3] - sv[4])
    u_fc = share_fc * v_cbf + (1.0 - share_fc) * v_cbc
    v_check = v_cc + u_fc
    v_bet = v_bf + v_bc
    u_root = share_root * v_check + (1.0 - share_root) * v_bet
    x_bet = w_cbf + w_cbc
    u_ac = share_ac * w_cc + (1.0 - share_ac) * x_bet
    u_fb = share_fb * w_bf + (1.0 - share_fb) * w_bc
    updates = (
        (ROOT_CHECK, v_check, u_root),
        (ROOT_BET, v_bet, u_root),
        (FC_FOLD, v_cbf, u_fc),
        (FC_CALL, v_cbc, u_fc),
        (AC_CHECK, w_cc, u_ac),
        (AC_BET, x_bet, u_ac),
        (FB_FOLD, w_bf, u_fb),
        (FB_CALL, w_bc, u_fb),
    )
    for row, value, node in updates:
        regret_out[row] = jnp.maximum(regrets[row] + value - node, 0.0)
    cont_ref[...] = jnp.sum(share_ref[...] * u_root, axis=0, keepdims=True)


def run_step(step, *operands):
    slots, width = operands[1].shape
    vmem = pl.BlockSpec(memory_space=pltpu.VMEM)
    return pl.pallas_call(
        functools.partial(step_kernel, step),
        out_shape=(
            jax.ShapeDtypeStruct((8, slots, width), jnp.float32),
            jax.ShapeDtypeStruct((6, slots, width), jnp.float32),
            jax.ShapeDtypeStruct((1, width), jnp.float32),
        ),
        in_specs=[vmem] * len(operands),
        out_specs=(vmem,) * 3,
        scratch_shapes=[
            pltpu.VMEM((width, width), jnp.bfloat16),
            pltpu.VMEM((slots, 8, width), jnp.float32),
            pltpu.VMEM((slots, 8, width), jnp.float32),
            pltpu.VMEM((slots, 8, width), jnp.float32),
        ],
        compiler_params=pltpu.CompilerParams(vmem_limit_bytes=56 * 1024 * 1024),
        cost_estimate=pl.CostEstimate(
            flops=16 * slots * width * width,
            bytes_accessed=2 * slots * width * width,
            transcendentals=0,
        ),
    )(*operands)


def sum_kernel(
    groups, shards, part_ref, out_ref, first, middle, second, sent1, came1, sent2, came2
):
    spots = (("inf", lax.axis_index("inf"), shards), ("grp", lax.axis_index("grp"), groups))
    barrier = pltpu.get_barrier_semaphore()
    for axis, spot, size in spots:
        for hop in range(1, size):
            pl.semaphore_signal(
                barrier,
                inc=1,
                device_id={axis: lax.rem(spot + hop, size)},
                device_id_type=pl.DeviceIdType.MESH,
            )
    pl.semaphore_wait(barrier, groups + shards - 2)

    def exchange(axis, spot, size, source, slots, sent, came):
        def move(hop, slot, target):
            return pltpu.make_async_remote_copy(
                src_ref=source,
                dst_ref=slots.at[slot],
                send_sem=sent.at[hop],
                recv_sem=came.at[slot],
                device_id={axis: target},
                device_id_type=pl.DeviceIdType.MESH,
            )

        for hop in range(1, size):
            move(hop, spot, lax.rem(spot + hop, size)).start()
        slots[spot] = source[...]
        for hop in range(1, size):
            sender = lax.rem(spot + size - hop, size)
            move(hop, sender, sender).wait_recv()
        total = slots[0]
        for slot in range(1, size):
            total = total + slots[slot]
        for hop in range(1, size):
            move(hop, spot, lax.rem(spot + hop, size)).wait_send()
        return total

    middle[...] = exchange(*spots[0], part_ref, first, sent1, came1)
    out_ref[...] = exchange(*spots[1], middle, second, sent2, came2)


def sum_all(part, groups, shards):
    vmem = pl.BlockSpec(memory_space=pltpu.VMEM)
    return pl.pallas_call(
        functools.partial(sum_kernel, groups, shards),
        out_shape=jax.ShapeDtypeStruct(part.shape, part.dtype),
        in_specs=[vmem],
        out_specs=vmem,
        scratch_shapes=[
            pltpu.VMEM((shards,) + part.shape, part.dtype),
            pltpu.VMEM(part.shape, part.dtype),
            pltpu.VMEM((groups,) + part.shape, part.dtype),
            pltpu.SemaphoreType.DMA((shards,)),
            pltpu.SemaphoreType.DMA((shards,)),
            pltpu.SemaphoreType.DMA((groups,)),
            pltpu.SemaphoreType.DMA((groups,)),
        ],
        compiler_params=pltpu.CompilerParams(collective_id=0, has_side_effects=True),
        cost_estimate=pl.CostEstimate(flops=0, bytes_accessed=30_000_000, transcendentals=0),
    )(part)


def last_kernel(total_weight, live_ref, one_ref, two_ref, regret_ref, turn_ref, out_ref):
    regrets = [regret_ref[row] for row in range(8)]
    unused, cols = reaches(regrets, one_ref[...], two_ref[...], live_ref[...])
    for row, term in enumerate(turn_rows(cols)):
        out_ref[row] = (turn_ref[row] + float(ITERS) * term) / total_weight


def on_device(range_one, range_two, flop_weight, board_mask, runout, strength):
    groups = lax.axis_size("grp")
    shards = lax.axis_size("inf")
    shard_id = lax.axis_index("inf")
    group_id = lax.axis_index("grp")
    low_table, high_table = hand_cards(H, HANDS)
    low_all = jnp.asarray(low_table)
    high_all = jnp.asarray(high_table)
    capacity = strength.shape[0]
    hand_block = strength.shape[2]
    flop_total = 12.0 * FLOP_GRP * groups
    rounds = ITERS - 1
    local_count = FLOP_GRP // shards

    small = jnp.concatenate(
        [flop_weight[:, None], runout[:, :rounds].reshape(capacity, 2 * rounds)], axis=1
    )
    small_all = lax.all_gather(small, "grp", axis=0, tiled=False)
    counts = jnp.sum((small_all[:, :, 0] > 0).astype(jnp.int32), axis=1, dtype=jnp.int32)
    rows = jnp.arange(capacity)
    group_ids = jnp.arange(groups)
    earlier = (group_ids[None, :] < group_ids[:, None]).astype(jnp.int32)
    place = jnp.sum(
        jnp.minimum(counts[None, None, :], rows[None, :, None] + earlier[:, None, :]),
        axis=2,
        dtype=jnp.int32,
    )
    place = jnp.where(rows[None, :] < counts[:, None], place, -1)

    own_place = jnp.sum(
        jnp.where(group_ids[:, None] == group_id, place, 0), axis=0, dtype=jnp.int32
    )
    target = jnp.arange(groups * FLOP_GRP)
    match = own_place[None, :] == target[:, None]
    is_valid = jnp.any(match, axis=1)
    source = jnp.sum(jnp.where(match, rows[None, :], 0), axis=1, dtype=jnp.int32)

    masked = jnp.where(board_mask[:, None, :] == 1, strength[:, :rounds], -1)
    masked = masked.reshape(capacity, rounds * hand_block)
    taken = jnp.where(is_valid[:, None], jnp.take(masked, source, axis=0), 0)
    arrived = lax.all_to_all(
        taken.reshape(groups, FLOP_GRP, rounds * hand_block),
        "grp",
        split_axis=0,
        concat_axis=0,
        tiled=True,
    )
    key_rows = jnp.sum(arrived, axis=0, dtype=jnp.int32)

    def spread(rows_now):
        rows_now = rows_now.reshape(shards, local_count, -1)
        return lax.all_to_all(rows_now, "inf", split_axis=0, concat_axis=0, tiled=True)

    def join(whole):
        return jnp.transpose(whole, (1, 0, 2)).reshape(local_count, H)

    first_keys = spread(key_rows[:, :hand_block])
    later_rows, first_keys = lax.optimization_barrier((key_rows[:, hand_block:], first_keys))
    later = spread(later_rows)
    flop_keys = [join(first_keys)] + [
        join(later[:, :, spot * hand_block : (spot + 1) * hand_block])
        for spot in range(rounds - 1)
    ]

    here = group_id * FLOP_GRP + shard_id * local_count + jnp.arange(local_count)
    mine = place.reshape(1, -1) == here[:, None]
    small_here = jnp.sum(
        jnp.where(mine[:, :, None], small_all.reshape(1, groups * capacity, -1), 0),
        axis=1,
        dtype=jnp.int32,
    )
    flop_share = small_here[:, 0:1].astype(jnp.float32) / flop_total

    is_hand = (jnp.arange(H) < HANDS)[None, :]
    is_live = (flop_keys[0] >= 0) & is_hand
    live = is_live.astype(jnp.float32)
    compat = (low_all[:, None] != low_all[None, :]) & (low_all[:, None] != high_all[None, :])
    compat = compat & (high_all[:, None] != low_all[None, :])
    compat = compat & (high_all[:, None] != high_all[None, :])
    compat = compat.astype(jnp.bfloat16)

    two_row = range_two[None, :]
    pre_fold = jnp.zeros((1, H), jnp.float32)
    pre_cont = jnp.zeros((1, H), jnp.float32)
    pre_sum = jnp.zeros((1, H), jnp.float32)
    state = ()
    for step in range(rounds):
        share_pre = action_share(pre_cont, pre_fold)
        one_range = range_one[None, :] * share_pre
        turn_card = small_here[:, 1 + 2 * step : 2 + 2 * step]
        river_card = small_here[:, 2 + 2 * step : 3 + 2 * step]
        blocked = (low_all[None, :] == turn_card) | (low_all[None, :] == river_card)
        blocked = blocked | (high_all[None, :] == turn_card) | (high_all[None, :] == river_card)
        alive = (is_live & jnp.logical_not(blocked)).astype(jnp.float32)
        regrets, turn_sum, cont_part = run_step(
            step,
            compat,
            order_floats(jnp.maximum(flop_keys[step], 0)),
            live,
            alive,
            flop_share,
            one_range,
            two_row,
            *state,
        )
        state = (regrets, turn_sum)
        cont_value = sum_all(cont_part, groups, shards)
        u_pre = share_pre * cont_value + (1.0 - share_pre) * FOLD_VALUE
        pre_cont = jnp.maximum(pre_cont + cont_value - u_pre, 0.0)
        pre_fold = jnp.maximum(pre_fold + FOLD_VALUE - u_pre, 0.0)
        pre_sum = pre_sum + float(step + 1) * one_range
    total_weight = ITERS * (ITERS + 1) / 2.0
    one_range = range_one[None, :] * action_share(pre_cont, pre_fold)
    turn_final = pl.pallas_call(
        functools.partial(last_kernel, total_weight),
        out_shape=jax.ShapeDtypeStruct((6, local_count, H), jnp.float32),
        in_specs=[pl.BlockSpec(memory_space=pltpu.VMEM)] * 5,
        out_specs=pl.BlockSpec(memory_space=pltpu.VMEM),
    )(live, one_range, two_row, *state)
    turn_final = jnp.transpose(turn_final, (1, 0, 2))
    pre_sum = (pre_sum + float(ITERS) * one_range) / total_weight
    pre_block = lax.dynamic_slice_in_dim(pre_sum[0], shard_id * hand_block, hand_block)
    return (turn_final, pre_block)


def solution(mesh):
    in_specs = (P(), P(), P("grp"), P("grp", "inf"), P("grp", None, None), P("grp", None, "inf"))
    out_specs = (P(("grp", "inf"), None, None), P("inf"))
    return jax.shard_map(
        on_device, mesh=mesh, in_specs=in_specs, out_specs=out_specs, check_vma=False
    )
```
